32 devices in a mesh: slides: 2 (over y), rows: 8 (over z, x), cols: 2 (over core).
Axes of the slice: x: 2, y: 2, z: 4, core: 2. Of those that a mesh axis runs over, the one named last changes fastest.
Arguments:
- tokens: bfloat16 [512, 32, 512], P(('slides', 'cols'), 'rows'), parts along dimension 0, may hold values from -6 to 6
- norm_gain: float32 [512], replicated, may hold values from 0.5 to 1.5
- w_in: bfloat16 [512, 2048], replicated, may hold values from -0.25 to 0.25
- w_bc: bfloat16 [512, 64], replicated, may hold values from -0.046875 to 0.046875
- rate_row: float32 [16, 1024], replicated, may hold values from 0.002 to 0.08
- rate_col: float32 [16, 1024], replicated, may hold values from 0.002 to 0.08
- skip_gain: float32 [1024], replicated, may hold values from 0.5 to 1.5
- w_out: bfloat16 [1024, 512], replicated, may hold values from -0.1875 to 0.1875
Outputs:
- mixed: bfloat16 [512, 32, 512], P(('slides', 'cols'), 'rows'), parts along dimension 0
The draws below stay inside these ranges and needn't reach their ends.
There are 2 independent parts, one for each index of `slides`. The reference program is written for one: setup_inputs(seed, part) draws one part's arguments, and reference() takes and returns one part's arrays. A program takes and returns all parts, laid end to end along the dimension named above; an argument that names none is the same for every part. Nothing has to cross between parts.
All inputs are finite; a program needn't handle non-finite values.
Results may differ from the reference program's by a relative error of at most 0.013.
Values may be sent and summed in bfloat16 or wider, within the bound.
A program may use at most 64 MiB of HBM per device.

```python
import math
import jax
import jax.numpy as jnp
from jax import lax

D = 512
E = 1024
N = 16
H = 256
W = 32


def block_levels(stream_key, extent, split, least, top_value):
    factor_of = 1.0
    for position, parts in split:
        draws = jax.random.uniform(jax.random.fold_in(jax.random.fold_in(stream_key, 6), position), (parts,), jnp.float32, least / len(split), top_value / len(split))
        factor_of = factor_of * jnp.repeat(jnp.exp(draws), extent[position] // parts).reshape((-1,) + (1,) * (len(extent) - 1 - position))
    return factor_of


def centred(own_key, dims, deviation, limit, cuts=(), dtype=jnp.bfloat16):
    entries = jax.random.normal(own_key, dims, jnp.float32) * deviation
    if len(cuts) > 0:
        entries = block_levels(own_key, dims, cuts, -0.22, 0.18) * entries
    return jnp.clip(entries, min=-limit, max=limit).astype(dtype)


def setup_inputs(seed: int = 0, part: int = 0) -> dict:
    arg_keys = jax.random.split(jax.random.key(seed), 9)
    own_keys = jax.random.split(jax.random.fold_in(arg_keys[8], part), 9)
    tokens = centred(own_keys[0], (H, W, D), 1.0, 6.0, ((0, 2), (1, 8)))
    norm_gain = jnp.clip(1.0 + 0.1 * jax.random.normal(arg_keys[1], (D,), jnp.float32), 0.5, 1.5)
    w_in = centred(arg_keys[2], (D, 2 * E), D ** -0.5, 0.25)
    w_bc = centred(arg_keys[3], (D, 4 * N), (32 * D) ** -0.5, 0.046875)
    rate_row = jnp.clip(jnp.exp(jax.random.uniform(arg_keys[4], (N, E), jnp.float32, math.log(0.002), math.log(0.08))), 0.002, 0.08)
    rate_col = jnp.clip(jnp.exp(jax.random.uniform(arg_keys[5], (N, E), jnp.float32, math.log(0.002), math.log(0.08))), 0.002, 0.08)
    skip_gain = jnp.clip(jax.random.uniform(arg_keys[6], (E,), jnp.float32, 0.5, 1.5), 0.5, 1.5)
    w_out = centred(arg_keys[7], (E, D), E ** -0.5, 0.1875)
    return {"tokens": tokens, "norm_gain": norm_gain, "w_in": w_in, "w_bc": w_bc, "rate_row": rate_row, "rate_col": rate_col, "skip_gain": skip_gain, "w_out": w_out}


def run_scan(series, inject, readout, rate, skip_weight):
    decay_factor = jnp.exp(-rate)

    def advance(carried, inputs):
        value_now, inject_now, read_now = inputs
        carried = decay_factor[None] * carried + inject_now[:, :, None] * value_now[:, None, :]
        result = jnp.einsum('ine,in->ie', carried, read_now, precision=lax.Precision.HIGHEST) + skip_weight * value_now
        return (carried, result)
    start_state = jnp.zeros((series.shape[1], rate.shape[0], rate.shape[1]), jnp.float32)
    _, results = lax.scan(advance, start_state, (series, inject, readout))
    return results

def reference(tokens, norm_gain, w_in, w_bc, rate_row, rate_col, skip_gain, w_out):
    inner_width = w_out.shape[0]
    state_width = rate_row.shape[0]
    as_float = tokens.astype(jnp.float32)
    scale_now = lax.rsqrt(lax.optimization_barrier(jnp.mean(as_float * as_float, axis=-1, keepdims=True)) + 1e-05)
    normed = (as_float * scale_now * norm_gain).astype(jnp.bfloat16)
    project = jnp.dot(normed, w_in, preferred_element_type=jnp.float32)
    inputs_u = lax.optimization_barrier(project[..., :inner_width].astype(jnp.bfloat16)).astype(jnp.float32)
    gate_z = lax.optimization_barrier(project[..., inner_width:].astype(jnp.bfloat16)).astype(jnp.float32)
    mixers = lax.optimization_barrier(jnp.dot(normed, w_bc, preferred_element_type=jnp.float32).astype(jnp.bfloat16)).astype(jnp.float32)
    b_row = mixers[..., :state_width]
    c_row = mixers[..., state_width:2 * state_width]
    b_col = mixers[..., 2 * state_width:3 * state_width]
    c_col = mixers[..., 3 * state_width:]
    along_rows = run_scan(inputs_u.transpose(1, 0, 2), b_row.transpose(1, 0, 2), c_row.transpose(1, 0, 2), rate_row, skip_gain)
    along_rows = along_rows.transpose(1, 0, 2)
    row_mixed = lax.optimization_barrier(along_rows.astype(jnp.bfloat16)).astype(jnp.float32)
    col_mixed = run_scan(row_mixed, b_col, c_col, rate_col, 1.0)
    gated = (col_mixed * jax.nn.silu(gate_z)).astype(jnp.bfloat16)
    return jnp.dot(gated, w_out, preferred_element_type=jnp.float32).astype(jnp.bfloat16)
```

```python
import functools

import jax
import jax.numpy as jnp
from jax import lax
from jax.experimental import pallas as pl
from jax.experimental.pallas import tpu as pltpu
from jax.sharding import PartitionSpec as P

LANES = 128
VMEM_LIMIT = 56 * 1024 * 1024


def normalise(tokens, gain):
    as_float = tokens.astype(jnp.float32)
    scale_now = lax.rsqrt(jnp.mean(as_float * as_float, axis=-1, keepdims=True) + 1e-05)
    return (as_float * scale_now * gain).astype(jnp.bfloat16)


def spread_channels(ref, value, tiles):
    rows = value.shape[0]
    for t in range(tiles):
        ref[pl.ds(t, rows, stride=tiles), :] = value[:, t * LANES : (t + 1) * LANES]


def spread_vectors(ref, value, first, states):
    rows = value.shape[0]
    for n in range(states):
        ref[n, 0:rows, :] = jnp.broadcast_to(value[:, first + n : first + n + 1], (rows, LANES))


def scan_step(carried, decay, value, inject_ref, readout_ref, patch, start, tiles):
    new = []
    totals = [start, None]
    for n, state in enumerate(carried):
        inject = inject_ref[n, pl.ds(patch, tiles, stride=0), :]
        readout = readout_ref[n, pl.ds(patch, tiles, stride=0), :]
        state = decay[n] * state + inject * value
        term = readout * state
        totals[n % 2] = term if totals[n % 2] is None else totals[n % 2] + term
        new.append(state)
    return tuple(new), totals[0] + totals[1]


def row_kernel(states, items, steps, tok_ref, gain_ref, w_ref, wbc_ref, rate_ref, skip_ref,
               out_ref, u_ref, inject_ref, readout_ref, decay_ref, skip_tile):
    tiles = u_ref.shape[0] // tok_ref.shape[0]
    normed = normalise(tok_ref[...], gain_ref[...])
    mixers = jnp.dot(normed, wbc_ref[...], preferred_element_type=jnp.float32)
    mixers = mixers.astype(jnp.bfloat16).astype(jnp.float32)
    spread_vectors(inject_ref, mixers, 0, states)
    spread_vectors(readout_ref, mixers, states, states)
    width = 2 * LANES
    for k in range(tiles // 2):
        part = jnp.dot(normed, w_ref[:, k * width : (k + 1) * width],
                       preferred_element_type=jnp.float32)
        part = part.astype(jnp.bfloat16).astype(jnp.float32)
        for h in range(2):
            u_ref[pl.ds(2 * k + h, part.shape[0], stride=tiles), :] = part[:, h * LANES : (h + 1) * LANES]
    spread_channels(decay_ref, jnp.exp(-rate_ref[...]), tiles)
    spread_channels(skip_tile, skip_ref[...], tiles)
    decay = [decay_ref[n * tiles : (n + 1) * tiles, :] for n in range(states)]
    skip = skip_tile[...]
    group = 2 if items % 2 == 0 else 1
    zero = jnp.zeros((tiles, LANES), jnp.float32)

    def one_group(first, _):
        def one_step(j, carry):
            result = []
            for g in range(group):
                patch = (first * group + g) * steps + j
                value = u_ref[pl.ds(pl.multiple_of(patch * tiles, tiles), tiles), :]
                state, total = scan_step(carry[g], decay, value, inject_ref, readout_ref,
                                         patch, skip * value, tiles)
                out_ref[first * group + g, j] = total.astype(jnp.bfloat16)
                result.append(state)
            return tuple(result)

        lax.fori_loop(0, steps, one_step, tuple((zero,) * states for _ in range(group)))
        return 0

    lax.fori_loop(0, items // group, one_group, 0)


def row_stage(tok, gain, w_in, w_bc, rate, skip, inner):
    items, steps, width = tok.shape
    states = rate.shape[0]
    tiles = inner // LANES
    patches = items * steps
    whole = lambda *shape: pl.BlockSpec(shape, lambda i: (0,) * len(shape))
    return pl.pallas_call(
        functools.partial(row_kernel, states, items, steps),
        grid=(1,),
        in_specs=[
            whole(patches, width), whole(1, width), whole(width, inner),
            whole(width, w_bc.shape[1]), whole(states, inner), whole(1, inner),
        ],
        out_specs=whole(items, steps, tiles, LANES),
        out_shape=jax.ShapeDtypeStruct((items, steps, tiles, LANES), jnp.bfloat16),
        scratch_shapes=[
            pltpu.VMEM((patches * tiles, LANES), jnp.float32),
            pltpu.VMEM((states, patches + 8, LANES), jnp.float32),
            pltpu.VMEM((states, patches + 8, LANES), jnp.float32),
            pltpu.VMEM((states * tiles, LANES), jnp.float32),
            pltpu.VMEM((tiles, LANES), jnp.float32),
        ],
        compiler_params=pltpu.CompilerParams(vmem_limit_bytes=VMEM_LIMIT),
        name="row_stage",
    )(tok.reshape(patches, width), gain, w_in, w_bc, rate, skip)


def col_kernel(states, devices, cores, items, rm_ref, mix_ref, z_ref, rate_ref, wout_ref,
               out_ref, y_ref, inject_ref, readout_ref, decay_ref, gated_ref):
    tiles = rm_ref.shape[2]
    block = rm_ref.shape[0] // (devices * cores)
    mixers = mix_ref[...].astype(jnp.float32)
    spread_vectors(inject_ref, mixers, 0, states)
    spread_vectors(readout_ref, mixers, states, states)
    spread_channels(decay_ref, jnp.exp(-rate_ref[...]), tiles)
    decay = [decay_ref[n * tiles : (n + 1) * tiles, :] for n in range(states)]
    zero = jnp.zeros((tiles, LANES), jnp.float32)

    def one_block(k, carry):
        source = (k % devices * cores + k // devices) * block

        def one_step(s, carry):
            result = []
            for g in range(items):
                patch = (k * block + s) * items + g
                value = rm_ref[source + s, g].astype(jnp.float32)
                state, total = scan_step(carry[g], decay, value, inject_ref, readout_ref,
                                         patch, value, tiles)
                y_ref[pl.ds(pl.multiple_of(patch * tiles, tiles), tiles), :] = total
                result.append(state)
            return tuple(result)

        return lax.fori_loop(0, block, one_step, carry)

    lax.fori_loop(0, devices * cores, one_block, tuple((zero,) * states for _ in range(items)))
    patches = z_ref.shape[0]
    for t in range(tiles):
        gate = z_ref[:, t * LANES : (t + 1) * LANES].astype(jnp.float32)
        mixed = y_ref[pl.ds(t, patches, stride=tiles), :]
        gated_ref[:, t * LANES : (t + 1) * LANES] = (
            mixed * (gate / (1.0 + jnp.exp(-gate)))
        ).astype(jnp.bfloat16)
    out_ref[...] = jnp.dot(
        gated_ref[...], wout_ref[...], preferred_element_type=jnp.float32
    ).astype(jnp.bfloat16)


def col_stage(row_mixed, mixers, gate, rate, w_out, devices, cores):
    height, items, tiles, _ = row_mixed.shape
    states = rate.shape[0]
    patches = height * items
    inner, width = w_out.shape
    whole = lambda *shape: pl.BlockSpec(shape, lambda i: (0,) * len(shape))
    return pl.pallas_call(
        functools.partial(col_kernel, states, devices, cores, items),
        grid=(1,),
        in_specs=[
            whole(height, items, tiles, LANES), whole(patches, mixers.shape[1]),
            whole(patches, inner), whole(states, inner), whole(inner, width),
        ],
        out_specs=whole(patches, width),
        out_shape=jax.ShapeDtypeStruct((patches, width), jnp.bfloat16),
        scratch_shapes=[
            pltpu.VMEM((patches * tiles, LANES), jnp.float32),
            pltpu.VMEM((states, patches + 8, LANES), jnp.float32),
            pltpu.VMEM((states, patches + 8, LANES), jnp.float32),
            pltpu.VMEM((states * tiles, LANES), jnp.float32),
            pltpu.VMEM((patches, inner), jnp.bfloat16),
        ],
        compiler_params=pltpu.CompilerParams(vmem_limit_bytes=VMEM_LIMIT),
        name="col_stage",
    )(row_mixed, mixers, gate, rate, w_out)


def per_device(tokens, norm_gain, w_in, w_bc, rate_row, rate_col, skip_gain, w_out):
    inner = w_out.shape[0]
    states = rate_row.shape[0]
    width = tokens.shape[-1]
    devices, cores = lax.axis_size("rows"), lax.axis_size("cols")
    gain = norm_gain[None]
    by_row = lax.all_to_all(tokens, "rows", split_axis=0, concat_axis=1, tiled=True)
    by_col = lax.all_to_all(tokens, "cols", split_axis=1, concat_axis=0, tiled=True)
    row_mixed = row_stage(by_row, gain, w_in, w_bc, rate_row, skip_gain[None], inner)
    moved = lax.all_to_all(row_mixed, ("rows", "cols"), split_axis=1, concat_axis=0, tiled=True)
    normed = normalise(by_col.reshape(-1, width), gain)
    gate = jnp.dot(normed, w_in[:, inner:], preferred_element_type=jnp.float32).astype(jnp.bfloat16)
    mixers = jnp.dot(normed, w_bc[:, 2 * states :], preferred_element_type=jnp.float32).astype(jnp.bfloat16)
    mixed = col_stage(moved, mixers, gate, rate_col, w_out, devices, cores)
    mixed = mixed.reshape(by_col.shape[0], by_col.shape[1], -1)
    return lax.all_to_all(mixed, "cols", split_axis=0, concat_axis=1, tiled=True)


def solution(mesh):
    placed = (P(("slides", "cols"), "rows", None), P(), P(), P(), P(), P(), P(), P())
    return jax.shard_map(
        per_device,
        mesh=mesh,
        in_specs=placed,
        out_specs=P(("slides", "cols"), "rows", None),
        check_vma=False,
    )
```

```python
import functools

import jax
import jax.numpy as jnp
from jax import lax
from jax.experimental import pallas as pl
from jax.experimental.pallas import tpu as pltpu
from jax.sharding import PartitionSpec as P

LANES = 128
VMEM_LIMIT = 60 * 1024 * 1024
MESH = pl.DeviceIdType.MESH


def normalise(tokens, gain):
    as_float = tokens.astype(jnp.float32)
    scale_now = lax.rsqrt(jnp.mean(as_float * as_float, axis=-1, keepdims=True) + 1e-05)
    return (as_float * scale_now * gain).astype(jnp.bfloat16)


def spread_channels(ref, value, tiles):
    rows = value.shape[0]
    for t in range(tiles):
        ref[pl.ds(t, rows, stride=tiles), :] = value[:, t * LANES : (t + 1) * LANES]


def spread_vectors(ref, value, first, states, base):
    rows = value.shape[0]
    for n in range(states):
        ref[n, pl.ds(base, rows), :] = jnp.broadcast_to(
            value[:, first + n : first + n + 1], (rows, LANES)
        )


def scan_step(carried, decay, value, inject_ref, readout_ref, patch, start, tiles):
    new = []
    totals = [start, None]
    for n, state in enumerate(carried):
        inject = inject_ref[n, pl.ds(patch, tiles, stride=0), :]
        readout = readout_ref[n, pl.ds(patch, tiles, stride=0), :]
        state = decay[n] * state + inject * value
        term = readout * state
        totals[n % 2] = term if totals[n % 2] is None else totals[n % 2] + term
        new.append(state)
    return tuple(new), totals[0] + totals[1]


def layer_kernel(
    states, rows_n, cols_n, share, per_core,
    tok_ref, gain_ref, win_ref, wbc_ref, rrate_ref, crate_ref, skip_ref, wout_ref,
    out_ref,
    tcol, tin, rsend, rrecv, u_ref, rb_ref, rc_ref, cb_ref, cc_ref, z_ref, y_ref, gated_ref,
    rdecay, cdecay, skip_tile, stage, land, state_ref,
    tsend_sem, tin_sem, csend_sem, crecv_sem, rsend_sem, rrecv_sem, osend_sem, orecv_sem,
):
    group_n = rows_n * cols_n
    pieces = tok_ref.shape[1]
    chunks = tin.shape[0]
    width = tok_ref.shape[3]
    inner = wout_ref.shape[0]
    tiles = inner // LANES
    piece_len = share * per_core
    chunk_len = group_n * piece_len
    blocks = stage.shape[0]
    blocks_home = blocks // cols_n
    block_len = stage.shape[1]
    r, c = lax.axis_index("rows"), lax.axis_index("cols")
    me = r * cols_n + c

    def spot(g):
        return {"rows": g // cols_n, "cols": g % cols_n}

    barrier = pltpu.get_barrier_semaphore()

    def greet(g, _):
        @pl.when(g != me)
        def _():
            pl.semaphore_signal(barrier, inc=1, device_id=spot(g), device_id_type=MESH)
        return 0

    lax.fori_loop(0, group_n, greet, 0)
    spread_channels(rdecay, jnp.exp(-rrate_ref[...]), tiles)
    spread_channels(cdecay, jnp.exp(-crate_ref[...]), tiles)
    spread_channels(skip_tile, skip_ref[...], tiles)
    pl.semaphore_wait(barrier, group_n - 1)

    local_chunks = max(1, chunks // cols_n)
    per_chunk = pieces // local_chunks

    def piece_of(k):
        piece = k // per_chunk * per_chunk + (k % per_chunk + me) % per_chunk
        place = c * pieces + piece
        return piece, place // group_n, place % group_n

    def token_copy(k):
        piece, q, g = piece_of(k)
        return g, pltpu.make_async_remote_copy(
            src_ref=tok_ref.at[:, piece], dst_ref=tin.at[q, r],
            send_sem=tsend_sem.at[piece], recv_sem=tin_sem.at[q],
            device_id=spot(g), device_id_type=MESH,
        )

    def send_tokens(k, _):
        piece, q, g = piece_of(k)

        @pl.when(g == me)
        def _():
            pltpu.make_async_copy(tok_ref.at[:, piece], tin.at[q, r], tin_sem.at[q]).start()

        @pl.when(g != me)
        def _():
            token_copy(k)[1].start()
        return 0

    lax.fori_loop(0, pieces, send_tokens, 0)

    def column_copy(step):
        other = (c + step) % cols_n
        return pltpu.make_async_remote_copy(
            src_ref=tok_ref.at[other], dst_ref=tcol.at[c],
            send_sem=csend_sem.at[step], recv_sem=crecv_sem.at[step],
            device_id={"cols": other}, device_id_type=MESH,
        )

    for step in range(1, cols_n):
        column_copy(step).start()

    def gate_part(tokens, core):
        normed = normalise(tokens.astype(jnp.float32).reshape(-1, width), gain_ref[...])
        count = normed.shape[0]
        base = pl.multiple_of(core * count, count)
        mixers = jnp.dot(normed, wbc_ref[...], preferred_element_type=jnp.float32)
        mixers = mixers.astype(jnp.bfloat16).astype(jnp.float32)
        spread_vectors(cb_ref, mixers, 2 * states, states, base)
        spread_vectors(cc_ref, mixers, 3 * states, states, base)
        for k in range(0, inner, 2 * LANES):
            z_ref[pl.ds(base, count), k : k + 2 * LANES] = jnp.dot(
                normed, win_ref[:, inner + k : inner + k + 2 * LANES],
                preferred_element_type=jnp.float32,
            ).astype(jnp.bfloat16)

    gate_part(tok_ref[c], c)

    zero = jnp.zeros((tiles, LANES), jnp.float32)
    lanes = 2 if share % 2 == 0 else 1

    def result_copy(q, k):
        g = (me + k) % group_n
        return pltpu.make_async_remote_copy(
            src_ref=rsend.at[q, pl.ds(g * piece_len, piece_len)],
            dst_ref=rrecv.at[q, pl.ds(me * piece_len, piece_len)],
            send_sem=rsend_sem.at[q, k], recv_sem=rrecv_sem.at[q],
            device_id=spot(g), device_id_type=MESH,
        )

    def row_chunk(q, _):
        pltpu.make_async_copy(tin.at[q], tin.at[q], tin_sem.at[q]).wait()
        normed = normalise(tin[q].astype(jnp.float32).reshape(chunk_len, width), gain_ref[...])
        mixers = jnp.dot(normed, wbc_ref[...], preferred_element_type=jnp.float32)
        mixers = mixers.astype(jnp.bfloat16).astype(jnp.float32)
        spread_vectors(rb_ref, mixers, 0, states, 0)
        spread_vectors(rc_ref, mixers, states, states, 0)
        for k in range(0, tiles, 2):
            part = jnp.dot(normed, win_ref[:, k * LANES : (k + 2) * LANES],
                           preferred_element_type=jnp.float32)
            part = part.astype(jnp.bfloat16).astype(jnp.float32)
            for h in range(2):
                u_ref[pl.ds(k + h, chunk_len, stride=tiles), :] = part[:, h * LANES : (h + 1) * LANES]
        decay = [rdecay[n * tiles : (n + 1) * tiles, :] for n in range(states)]
        skip = skip_tile[...]

        def one_group(first, _):
            def one_step(j, carry):
                carry = list(carry)
                for w in range(per_core):
                    for b in range(lanes):
                        patch = (j * share + first * lanes + b) * per_core + w
                        value = u_ref[pl.ds(pl.multiple_of(patch * tiles, tiles), tiles), :]
                        carry[b], total = scan_step(carry[b], decay, value, rb_ref, rc_ref,
                                                    patch, skip * value, tiles)
                        rsend[q, patch] = total.astype(jnp.bfloat16)
                return tuple(carry)

            lax.fori_loop(0, group_n, one_step, tuple((zero,) * states for _ in range(lanes)))
            return 0

        lax.fori_loop(0, share // lanes, one_group, 0)

        def send_result(k, _):
            result_copy(q, k).start()
            return 0

        pltpu.make_async_copy(
            rsend.at[q, pl.ds(me * piece_len, piece_len)],
            rrecv.at[q, pl.ds(me * piece_len, piece_len)], rrecv_sem.at[q],
        ).start()
        lax.fori_loop(1, group_n, send_result, 0)
        return 0

    lax.fori_loop(0, chunks, row_chunk, 0)

    for step in range(1, cols_n):
        column_copy(step).wait_recv()
        source = (c + cols_n - step) % cols_n
        gate_part(tcol[source], source)

    for g in range(per_core):
        for n in range(states):
            state_ref[g, n] = zero

    def out_copy(o):
        return pltpu.make_async_remote_copy(
            src_ref=stage.at[o], dst_ref=land.at[c, o % blocks_home],
            send_sem=osend_sem.at[o], recv_sem=orecv_sem.at[c, o % blocks_home],
            device_id={"cols": o // blocks_home}, device_id_type=MESH,
        )

    def col_chunk(q, _):
        pltpu.make_async_copy(rrecv.at[q], rrecv.at[q], rrecv_sem.at[q]).wait()
        decay = [cdecay[n * tiles : (n + 1) * tiles, :] for n in range(states)]
        base = q * chunk_len

        def one_step(s, carry):
            result = []
            for g in range(per_core):
                patch = s * per_core + g
                value = rrecv[q, patch].astype(jnp.float32)
                state, total = scan_step(carry[g], decay, value, cb_ref, cc_ref,
                                         base + patch, value, tiles)
                y_ref[pl.ds(pl.multiple_of(patch * tiles, tiles), tiles), :] = total
                result.append(state)
            return tuple(result)

        carry = tuple(tuple(state_ref[g, n] for n in range(states)) for g in range(per_core))
        carry = lax.fori_loop(0, chunk_len // per_core, one_step, carry)
        for g in range(per_core):
            for n in range(states):
                state_ref[g, n] = carry[g][n]
        start = pl.multiple_of(base, chunk_len)
        for t in range(tiles):
            gate = z_ref[pl.ds(start, chunk_len), t * LANES : (t + 1) * LANES].astype(jnp.float32)
            mixed = y_ref[pl.ds(t, chunk_len, stride=tiles), :]
            gated_ref[:, t * LANES : (t + 1) * LANES] = (
                mixed * (gate / (1.0 + jnp.exp(-gate)))
            ).astype(jnp.bfloat16)
        result = jnp.dot(gated_ref[...], wout_ref[...], preferred_element_type=jnp.float32)
        result = result.astype(jnp.bfloat16)
        for k in range(blocks // chunks):
            o = q * (blocks // chunks) + k
            block = result[k * block_len : (k + 1) * block_len]
            stage[o] = block

            @pl.when(o // blocks_home == c)
            def _():
                land[c, o % blocks_home] = block

            @pl.when(o // blocks_home != c)
            def _():
                out_copy(o).start()
        return 0

    lax.fori_loop(0, chunks, col_chunk, 0)

    def drain_tokens(k, _):
        g, copy = token_copy(k)

        @pl.when(g != me)
        def _():
            copy.wait_send()
        return 0

    lax.fori_loop(0, pieces, drain_tokens, 0)
    for step in range(1, cols_n):
        column_copy(step).wait_send()

    def drain_results(q, _):
        def one(k, _):
            result_copy(q, k).wait_send()
            return 0
        return lax.fori_loop(1, group_n, one, 0)

    lax.fori_loop(0, chunks, drain_results, 0)

    def drain_out(o, _):
        @pl.when(o // blocks_home != c)
        def _():
            out_copy(o).wait_send()
        return 0

    lax.fori_loop(0, blocks, drain_out, 0)
    for source in range(cols_n):
        @pl.when(source != c)
        def _():
            for i in range(blocks_home):
                pltpu.make_async_copy(
                    land.at[source, i], land.at[source, i], orecv_sem.at[source, i]
                ).wait()
    out_ref[...] = land[...]


def per_device(tokens, norm_gain, w_in, w_bc, rate_row, rate_col, skip_gain, w_out):
    inner, width_out = w_out.shape
    states = rate_row.shape[0]
    height, columns, width = tokens.shape
    rows_n, cols_n = lax.axis_size("rows"), lax.axis_size("cols")
    group_n = rows_n * cols_n
    per_core = columns // cols_n
    total = height * cols_n
    share = min(4, total // group_n)
    chunks = total // (group_n * share)
    pieces = height // share
    piece_len = share * per_core
    chunk_len = group_n * piece_len
    tiles = inner // LANES
    blocks = max(chunks, cols_n)
    block_len = total * per_core // blocks
    patches = total * per_core
    arranged = tokens.reshape(height, cols_n, per_core, width).transpose(1, 0, 2, 3)
    arranged = arranged.reshape(cols_n, pieces, piece_len, width)
    f32, bf16 = jnp.float32, jnp.bfloat16
    dma = pltpu.SemaphoreType.DMA
    out = pl.pallas_call(
        functools.partial(layer_kernel, states, rows_n, cols_n, share, per_core),
        in_specs=[pl.BlockSpec(memory_space=pltpu.VMEM)] * 8,
        out_specs=pl.BlockSpec(memory_space=pltpu.VMEM),
        out_shape=jax.ShapeDtypeStruct((cols_n, blocks // cols_n, block_len, width_out), bf16),
        scratch_shapes=[
            pltpu.VMEM((cols_n, pieces, piece_len, width), bf16),
            pltpu.VMEM((chunks, rows_n, cols_n, piece_len, width), bf16),
            pltpu.VMEM((chunks, chunk_len, tiles, LANES), bf16),
            pltpu.VMEM((chunks, chunk_len, tiles, LANES), bf16),
            pltpu.VMEM((chunk_len * tiles, LANES), f32),
            pltpu.VMEM((states, chunk_len + 8, LANES), f32),
            pltpu.VMEM((states, chunk_len + 8, LANES), f32),
            pltpu.VMEM((states, patches + 8, LANES), f32),
            pltpu.VMEM((states, patches + 8, LANES), f32),
            pltpu.VMEM((patches, inner), bf16),
            pltpu.VMEM((chunk_len * tiles, LANES), f32),
            pltpu.VMEM((chunk_len, inner), bf16),
            pltpu.VMEM((states * tiles, LANES), f32),
            pltpu.VMEM((states * tiles, LANES), f32),
            pltpu.VMEM((tiles, LANES), f32),
            pltpu.VMEM((blocks, block_len, width_out), bf16),
            pltpu.VMEM((cols_n, blocks // cols_n, block_len, width_out), bf16),
            pltpu.VMEM((per_core, states, tiles, LANES), f32),
            dma((pieces,)), dma((chunks,)), dma((cols_n,)), dma((cols_n,)),
            dma((chunks, group_n)), dma((chunks,)), dma((blocks,)),
            dma((cols_n, blocks // cols_n)),
        ],
        compiler_params=pltpu.CompilerParams(
            vmem_limit_bytes=VMEM_LIMIT, collective_id=0, has_side_effects=True
        ),
        name="layer",
    )(arranged, norm_gain[None], w_in, w_bc, rate_row, rate_col, skip_gain[None], w_out)
    out = out.reshape(cols_n, height, per_core, width_out).transpose(1, 0, 2, 3)
    return out.reshape(height, columns, width_out)


def solution(mesh):
    placed = (P(("slides", "cols"), "rows", None), P(), P(), P(), P(), P(), P(), P())
    return jax.shard_map(
        per_device,
        mesh=mesh,
        in_specs=placed,
        out_specs=P(("slides", "cols"), "rows", None),
        check_vma=False,
    )
```

```python
import functools

import jax
import jax.numpy as jnp
from jax import lax
from jax.experimental import pallas as pl
from jax.experimental.pallas import tpu as pltpu
from jax.sharding import PartitionSpec as P

LANES = 128
VMEM_LIMIT = 60 * 1024 * 1024
MESH = pl.DeviceIdType.MESH


def normalise(tokens, gain):
    as_float = tokens.astype(jnp.float32)
    scale_now = lax.rsqrt(jnp.mean(as_float * as_float, axis=-1, keepdims=True) + 1e-05)
    return (as_float * scale_now * gain).astype(jnp.bfloat16)


def transposed_dot(a, b):
    return lax.dot_general(a, b, (((1,), (1,)), ((), ())), preferred_element_type=jnp.float32)


def spread_channels(ref, value, tiles):
    rows = value.shape[0]
    for t in range(tiles):
        ref[pl.ds(t, rows, stride=tiles), :] = value[:, t * LANES : (t + 1) * LANES]


def spread_vectors(ref, value, first, states, base):
    rows = value.shape[0]
    for n in range(states):
        ref[n, pl.ds(base, rows), :] = jnp.broadcast_to(
            value[:, first + n : first + n + 1], (rows, LANES)
        )


def scan_step(carried, decay, value, inject_ref, readout_ref, patch, start, tiles):
    new = []
    totals = [start, None]
    for n, state in enumerate(carried):
        inject = inject_ref[n, pl.ds(patch, tiles, stride=0), :]
        readout = readout_ref[n, pl.ds(patch, tiles, stride=0), :]
        state = decay[n] * state + inject * value
        term = readout * state
        totals[n % 2] = term if totals[n % 2] is None else totals[n % 2] + term
        new.append(state)
    return tuple(new), totals[0] + totals[1]


def layer_kernel(
    states, rows_n, cols_n, share, per_core,
    tok_ref, gain_in, win_in, wbc_in, rrate_in, crate_in, skip_in, wout_in,
    out_ref,
    gain_ref, win_ref, wbc_ref, rrate_ref, crate_ref, skip_ref, wout_ref, tcol, tin, rsend, rrecv, u_ref, rb_ref, rc_ref, cb_ref, cc_ref, z_ref, y_ref, gated_ref,
    rdecay, cdecay, skip_tile, stage, land, state_ref,
    tsend_sem, tin_sem, csend_sem, crecv_sem, rsend_sem, rrecv_sem, osend_sem, orecv_sem, fetch_sem,
):
    group_n = rows_n * cols_n
    pieces = tok_ref.shape[0] // share
    chunks = tin.shape[0]
    columns, width = tok_ref.shape[1:]
    inner = wout_ref.shape[0]
    tiles = inner // LANES
    piece_len = share * per_core
    chunk_len = group_n * piece_len
    blocks = stage.shape[0]
    blocks_home = blocks // cols_n
    block_len = stage.shape[1]
    r, c = lax.axis_index("rows"), lax.axis_index("cols")
    me = r * cols_n + c

    def spot(g):
        return {"rows": g // cols_n, "cols": g % cols_n}

    barrier = pltpu.get_barrier_semaphore()

    def greet(g, _):
        @pl.when(g != me)
        def _():
            pl.semaphore_signal(barrier, inc=1, device_id=spot(g), device_id_type=MESH)
        return 0

    lax.fori_loop(0, group_n, greet, 0)
    fetches = [
        pltpu.make_async_copy(src, dst, fetch_sem.at[k])
        for k, (src, dst) in enumerate((
            (rrate_in, rrate_ref), (crate_in, crate_ref), (skip_in, skip_ref), (gain_in, gain_ref),
            (wbc_in, wbc_ref), (tok_ref, tcol.at[c]), (win_in, win_ref), (wout_in, wout_ref),
        ))
    ]
    for fetch in fetches:
        fetch.start()
    pl.semaphore_wait(barrier, group_n - 1)

    local_chunks = max(1, chunks // cols_n)
    per_chunk = pieces // local_chunks

    def piece_of(k):
        piece = k // per_chunk * per_chunk + (k % per_chunk + me) % per_chunk
        place = c * pieces + piece
        return piece, place // group_n, place % group_n

    def token_copy(k):
        piece, q, g = piece_of(k)
        return g, pltpu.make_async_remote_copy(
            src_ref=tok_ref.at[pl.ds(piece * share, share)], dst_ref=tin.at[q, r],
            send_sem=tsend_sem.at[piece], recv_sem=tin_sem.at[q],
            device_id=spot(g), device_id_type=MESH,
        )

    def send_tokens(k, _):
        piece, q, g = piece_of(k)

        @pl.when(g == me)
        def _():
            pltpu.make_async_copy(tok_ref.at[pl.ds(piece * share, share)], tin.at[q, r], tin_sem.at[q]).start()

        @pl.when(g != me)
        def _():
            token_copy(k)[1].start()
        return 0

    lax.fori_loop(0, pieces, send_tokens, 0)

    def column_copy(step):
        other = (c + step) % cols_n
        return pltpu.make_async_remote_copy(
            src_ref=tok_ref, dst_ref=tcol.at[c],
            send_sem=csend_sem.at[step], recv_sem=crecv_sem.at[step],
            device_id={"cols": other}, device_id_type=MESH,
        )

    for step in range(1, cols_n):
        column_copy(step).start()

    def gate_part(tokens, core):
        tokens = tokens.astype(jnp.float32)
        own = tokens[:, :per_core]
        for k in range(1, cols_n):
            own = jnp.where(c == k, tokens[:, k * per_core : (k + 1) * per_core], own)
        normed = normalise(own.reshape(-1, width), gain_ref[...])
        count = normed.shape[0]
        base = pl.multiple_of(core * count, count)
        mixers = transposed_dot(normed, wbc_ref[...])
        mixers = mixers.astype(jnp.bfloat16).astype(jnp.float32)
        spread_vectors(cb_ref, mixers, 2 * states, states, base)
        spread_vectors(cc_ref, mixers, 3 * states, states, base)
        for k in range(0, inner, 2 * LANES):
            z_ref[pl.ds(base, count), k : k + 2 * LANES] = jnp.dot(
                normed, win_ref[:, inner + k : inner + k + 2 * LANES],
                preferred_element_type=jnp.float32,
            ).astype(jnp.bfloat16)

    for fetch in fetches:
        fetch.wait()
    spread_channels(rdecay, jnp.exp(-rrate_ref[...]), tiles)
    spread_channels(cdecay, jnp.exp(-crate_ref[...]), tiles)
    spread_channels(skip_tile, skip_ref[...], tiles)
    gate_part(tcol[c], c)

    zero = jnp.zeros((tiles, LANES), jnp.float32)
    lanes = 2 if share % 2 == 0 else 1

    def result_copy(q, k):
        g = (me + k) % group_n
        return pltpu.make_async_remote_copy(
            src_ref=rsend.at[q, pl.ds(g * piece_len, piece_len)],
            dst_ref=rrecv.at[q, pl.ds(me * piece_len, piece_len)],
            send_sem=rsend_sem.at[q, k], recv_sem=rrecv_sem.at[q],
            device_id=spot(g), device_id_type=MESH,
        )

    def row_chunk(q, _):
        pltpu.make_async_copy(tin.at[q], tin.at[q], tin_sem.at[q]).wait()
        normed = normalise(tin[q].astype(jnp.float32).reshape(chunk_len, width), gain_ref[...])
        mixers = transposed_dot(normed, wbc_ref[...])
        mixers = mixers.astype(jnp.bfloat16).astype(jnp.float32)
        spread_vectors(rb_ref, mixers, 0, states, 0)
        spread_vectors(rc_ref, mixers, states, states, 0)
        for k in range(0, tiles, 2):
            part = jnp.dot(normed, win_ref[:, k * LANES : (k + 2) * LANES],
                           preferred_element_type=jnp.float32)
            part = part.astype(jnp.bfloat16).astype(jnp.float32)
            for h in range(2):
                u_ref[pl.ds(k + h, chunk_len, stride=tiles), :] = part[:, h * LANES : (h + 1) * LANES]
        decay = [rdecay[n * tiles : (n + 1) * tiles, :] for n in range(states)]
        skip = skip_tile[...]

        def one_group(first, _):
            def one_step(j, carry):
                carry = list(carry)
                for w in range(columns):
                    for b in range(lanes):
                        row = first * lanes + b
                        patch = (j * share + row) * columns + w
                        owner = j * cols_n + w // per_core
                        value = u_ref[pl.ds(pl.multiple_of(patch * tiles, tiles), tiles), :]
                        carry[b], total = scan_step(carry[b], decay, value, rb_ref, rc_ref,
                                                    patch, skip * value, tiles)
                        rsend[q, (owner * share + row) * per_core + w % per_core] = total.astype(jnp.bfloat16)
                return tuple(carry)

            lax.fori_loop(0, rows_n, one_step, tuple((zero,) * states for _ in range(lanes)))
            return 0

        lax.fori_loop(0, share // lanes, one_group, 0)

        def send_result(k, _):
            result_copy(q, k).start()
            return 0

        pltpu.make_async_copy(
            rsend.at[q, pl.ds(me * piece_len, piece_len)],
            rrecv.at[q, pl.ds(me * piece_len, piece_len)], rrecv_sem.at[q],
        ).start()
        lax.fori_loop(1, group_n, send_result, 0)
        return 0

    lax.fori_loop(0, chunks, row_chunk, 0)

    for step in range(1, cols_n):
        column_copy(step).wait_recv()
        source = (c + cols_n - step) % cols_n
        gate_part(tcol[source], source)

    for g in range(per_core):
        for n in range(states):
            state_ref[g, n] = zero

    def out_copy(o):
        return pltpu.make_async_remote_copy(
            src_ref=stage.at[o], dst_ref=land.at[c, o % blocks_home],
            send_sem=osend_sem.at[o], recv_sem=orecv_sem.at[c, o % blocks_home],
            device_id={"cols": o // blocks_home}, device_id_type=MESH,
        )

    def col_chunk(q, _):
        pltpu.make_async_copy(rrecv.at[q], rrecv.at[q], rrecv_sem.at[q]).wait()
        decay = [cdecay[n * tiles : (n + 1) * tiles, :] for n in range(states)]
        base = q * chunk_len

        def one_step(s, carry):
            result = []
            for g in range(per_core):
                patch = s * per_core + g
                value = rrecv[q, patch].astype(jnp.float32)
                state, total = scan_step(carry[g], decay, value, cb_ref, cc_ref,
                                         base + patch, value, tiles)
                y_ref[pl.ds(pl.multiple_of(patch * tiles, tiles), tiles), :] = total
                result.append(state)
            return tuple(result)

        carry = tuple(tuple(state_ref[g, n] for n in range(states)) for g in range(per_core))
        carry = lax.fori_loop(0, chunk_len // per_core, one_step, carry)
        for g in range(per_core):
            for n in range(states):
                state_ref[g, n] = carry[g][n]
        start = pl.multiple_of(base, chunk_len)
        for t in range(tiles):
            gate = z_ref[pl.ds(start, chunk_len), t * LANES : (t + 1) * LANES].astype(jnp.float32)
            mixed = y_ref[pl.ds(t, chunk_len, stride=tiles), :]
            gated_ref[:, t * LANES : (t + 1) * LANES] = (
                mixed * (gate / (1.0 + jnp.exp(-gate)))
            ).astype(jnp.bfloat16)
        result = jnp.dot(gated_ref[...], wout_ref[...], preferred_element_type=jnp.float32)
        result = result.astype(jnp.bfloat16)
        for k in range(blocks // chunks):
            o = q * (blocks // chunks) + k
            block = result[k * block_len : (k + 1) * block_len]
            stage[o] = block

            @pl.when(o // blocks_home == c)
            def _():
                land[c, o % blocks_home] = block

            @pl.when(o // blocks_home != c)
            def _():
                out_copy(o).start()
        return 0

    lax.fori_loop(0, chunks, col_chunk, 0)

    def drain_tokens(k, _):
        g, copy = token_copy(k)

        @pl.when(g != me)
        def _():
            copy.wait_send()
        return 0

    lax.fori_loop(0, pieces, drain_tokens, 0)
    for step in range(1, cols_n):
        column_copy(step).wait_send()

    def drain_results(q, _):
        def one(k, _):
            result_copy(q, k).wait_send()
            return 0
        return lax.fori_loop(1, group_n, one, 0)

    lax.fori_loop(0, chunks, drain_results, 0)

    def drain_out(o, _):
        @pl.when(o // blocks_home != c)
        def _():
            out_copy(o).wait_send()
        return 0

    lax.fori_loop(0, blocks, drain_out, 0)
    for source in range(cols_n):
        @pl.when(source != c)
        def _():
            for i in range(blocks_home):
                pltpu.make_async_copy(
                    land.at[source, i], land.at[source, i], orecv_sem.at[source, i]
                ).wait()
    for i in range(blocks_home):
        parts = [
            land[s, i].astype(jnp.float32).reshape(block_len // per_core, per_core, -1)
            for s in range(cols_n)
        ]
        rows = block_len // per_core
        out_ref[i * rows : (i + 1) * rows] = jnp.concatenate(parts, axis=1).astype(jnp.bfloat16)


def per_device(tokens, norm_gain, w_in, w_bc, rate_row, rate_col, skip_gain, w_out):
    inner, width_out = w_out.shape
    states = rate_row.shape[0]
    height, columns, width = tokens.shape
    rows_n, cols_n = lax.axis_size("rows"), lax.axis_size("cols")
    group_n = rows_n * cols_n
    per_core = columns // cols_n
    total = height * cols_n
    share = min(2, total // group_n)
    chunks = total // (group_n * share)
    pieces = height // share
    piece_len = share * per_core
    chunk_len = group_n * piece_len
    tiles = inner // LANES
    blocks = max(chunks, cols_n)
    block_len = total * per_core // blocks
    patches = total * per_core
    f32, bf16 = jnp.float32, jnp.bfloat16
    dma = pltpu.SemaphoreType.DMA
    out = pl.pallas_call(
        functools.partial(layer_kernel, states, rows_n, cols_n, share, per_core),
        in_specs=[pl.BlockSpec(memory_space=pl.ANY)] * 8,
        out_specs=pl.BlockSpec(memory_space=pltpu.VMEM),
        out_shape=jax.ShapeDtypeStruct((height, columns, width_out), bf16),
        scratch_shapes=[
            pltpu.VMEM((1, width), f32),
            pltpu.VMEM(w_in.shape, bf16),
            pltpu.VMEM(w_bc.shape[::-1], bf16),
            pltpu.VMEM(rate_row.shape, f32),
            pltpu.VMEM(rate_col.shape, f32),
            pltpu.VMEM((1, inner), f32),
            pltpu.VMEM(w_out.shape, bf16),
            pltpu.VMEM((cols_n, height, columns, width), bf16),
            pltpu.VMEM((chunks, rows_n, share, columns, width), bf16),
            pltpu.VMEM((chunks, chunk_len, tiles, LANES), bf16),
            pltpu.VMEM((chunks, chunk_len, tiles, LANES), bf16),
            pltpu.VMEM((chunk_len * tiles, LANES), f32),
            pltpu.VMEM((states, chunk_len + 8, LANES), f32),
            pltpu.VMEM((states, chunk_len + 8, LANES), f32),
            pltpu.VMEM((states, patches + 8, LANES), f32),
            pltpu.VMEM((states, patches + 8, LANES), f32),
            pltpu.VMEM((patches, inner), bf16),
            pltpu.VMEM((chunk_len * tiles, LANES), f32),
            pltpu.VMEM((chunk_len, inner), bf16),
            pltpu.VMEM((states * tiles, LANES), f32),
            pltpu.VMEM((states * tiles, LANES), f32),
            pltpu.VMEM((tiles, LANES), f32),
            pltpu.VMEM((blocks, block_len, width_out), bf16),
            pltpu.VMEM((cols_n, blocks // cols_n, block_len, width_out), bf16),
            pltpu.VMEM((per_core, states, tiles, LANES), f32),
            dma((pieces,)), dma((chunks,)), dma((cols_n,)), dma((cols_n,)),
            dma((chunks, group_n)), dma((chunks,)), dma((blocks,)),
            dma((cols_n, blocks // cols_n)), dma((8,)),
        ],
        compiler_params=pltpu.CompilerParams(
            vmem_limit_bytes=VMEM_LIMIT, collective_id=0, has_side_effects=True
        ),
        name="layer",
    )(tokens, norm_gain[None], w_in, w_bc.T, rate_row, rate_col, skip_gain[None], w_out)
    return out


def solution(mesh):
    placed = (P(("slides", "cols"), "rows", None), P(), P(), P(), P(), P(), P(), P())
    return jax.shard_map(
        per_device,
        mesh=mesh,
        in_specs=placed,
        out_specs=P(("slides", "cols"), "rows", None),
        check_vma=False,
    )
```

```python
import functools

import jax
import jax.numpy as jnp
from jax import lax
from jax.experimental import pallas as pl
from jax.experimental.pallas import tpu as pltpu
from jax.sharding import PartitionSpec as P

LANES = 128
VMEM_LIMIT = 60 * 1024 * 1024
MESH = pl.DeviceIdType.MESH


def normalise(tokens, gain):
    as_float = tokens.astype(jnp.float32)
    scale_now = lax.rsqrt(jnp.mean(as_float * as_float, axis=-1, keepdims=True) + 1e-05)
    return (as_float * scale_now * gain).astype(jnp.bfloat16)


def transposed_dot(a, b):
    return lax.dot_general(a, b, (((1,), (1,)), ((), ())), preferred_element_type=jnp.float32)


def spread_channels(ref, value, tiles):
    rows = value.shape[0]
    for t in range(tiles):
        ref[pl.ds(t, rows, stride=tiles), :] = value[:, t * LANES : (t + 1) * LANES]


def spread_vectors(ref, value, first, states, base):
    rows = value.shape[0]
    for n in range(states):
        ref[n, pl.ds(base, rows), :] = jnp.broadcast_to(
            value[:, first + n : first + n + 1], (rows, LANES)
        )


def scan_step(carried, decay, value, inject_ref, readout_ref, patch, start, tiles):
    new = []
    totals = [start, None]
    for n, state in enumerate(carried):
        inject = inject_ref[n, pl.ds(patch, tiles, stride=0), :]
        readout = readout_ref[n, pl.ds(patch, tiles, stride=0), :]
        state = decay[n] * state + inject * value
        term = readout * state
        totals[n % 2] = term if totals[n % 2] is None else totals[n % 2] + term
        new.append(state)
    return tuple(new), totals[0] + totals[1]


def layer_kernel(
    states, rows_n, cols_n, share, per_core,
    tok_ref, gain_in, win_in, wbc_in, rrate_in, crate_in, skip_in, wout_in,
    out_ref,
    gain_ref, win_ref, wbc_ref, rrate_ref, crate_ref, skip_ref, wout_ref, tcol, tin, rsend, rrecv, u_ref, rb_ref, rc_ref, cb_ref, cc_ref, z_ref, y_ref, gated_ref,
    rdecay, cdecay, skip_tile, stage, land, state_ref,
    tsend_sem, tin_sem, csend_sem, crecv_sem, rsend_sem, rrecv_sem, osend_sem, orecv_sem, fetch_sem,
):
    group_n = rows_n * cols_n
    pieces = tok_ref.shape[0] // share
    chunks = tin.shape[0]
    columns, width = tok_ref.shape[1:]
    inner = wout_ref.shape[0]
    tiles = inner // LANES
    piece_len = share * per_core
    chunk_len = group_n * piece_len
    blocks = stage.shape[0]
    blocks_home = blocks // cols_n
    block_len = stage.shape[1]
    r, c = lax.axis_index("rows"), lax.axis_index("cols")
    me = r * cols_n + c

    def spot(g):
        return {"rows": g // cols_n, "cols": g % cols_n}

    barrier = pltpu.get_barrier_semaphore()

    def greet(g, _):
        @pl.when(g != me)
        def _():
            pl.semaphore_signal(barrier, inc=1, device_id=spot(g), device_id_type=MESH)
        return 0

    lax.fori_loop(0, group_n, greet, 0)
    fetches = [
        pltpu.make_async_copy(src, dst, fetch_sem.at[k])
        for k, (src, dst) in enumerate((
            (rrate_in, rrate_ref), (crate_in, crate_ref), (skip_in, skip_ref), (gain_in, gain_ref),
            (wbc_in, wbc_ref), (tok_ref, tcol.at[c]), (win_in, win_ref), (wout_in, wout_ref),
        ))
    ]
    for fetch in fetches:
        fetch.start()
    pl.semaphore_wait(barrier, group_n - 1)

    local_chunks = max(1, chunks // cols_n)
    per_chunk = pieces // local_chunks

    def piece_of(k):
        piece = k // per_chunk * per_chunk + (k % per_chunk + me) % per_chunk
        place = c * pieces + piece
        return piece, place // group_n, place % group_n

    def token_copy(k):
        piece, q, g = piece_of(k)
        return g, pltpu.make_async_remote_copy(
            src_ref=tok_ref.at[pl.ds(piece * share, share)], dst_ref=tin.at[q, r],
            send_sem=tsend_sem.at[piece], recv_sem=tin_sem.at[q],
            device_id=spot(g), device_id_type=MESH,
        )

    def send_tokens(k, _):
        piece, q, g = piece_of(k)

        @pl.when(g == me)
        def _():
            pltpu.make_async_copy(tok_ref.at[pl.ds(piece * share, share)], tin.at[q, r], tin_sem.at[q]).start()

        @pl.when(g != me)
        def _():
            token_copy(k)[1].start()
        return 0

    lax.fori_loop(0, pieces, send_tokens, 0)

    def column_copy(step):
        other = (c + step) % cols_n
        return pltpu.make_async_remote_copy(
            src_ref=tok_ref, dst_ref=tcol.at[c],
            send_sem=csend_sem.at[step], recv_sem=crecv_sem.at[step],
            device_id={"cols": other}, device_id_type=MESH,
        )

    for step in range(1, cols_n):
        column_copy(step).start()

    def gate_part(tokens, core):
        tokens = tokens.astype(jnp.float32)
        own = tokens[:, :per_core]
        for k in range(1, cols_n):
            own = jnp.where(c == k, tokens[:, k * per_core : (k + 1) * per_core], own)
        normed = normalise(own.reshape(-1, width), gain_ref[...])
        count = normed.shape[0]
        base = pl.multiple_of(core * count, count)
        mixers = transposed_dot(normed, wbc_ref[...])
        mixers = mixers.astype(jnp.bfloat16).astype(jnp.float32)
        spread_vectors(cb_ref, mixers, 2 * states, states, base)
        spread_vectors(cc_ref, mixers, 3 * states, states, base)
        for k in range(0, inner, 2 * LANES):
            z_ref[pl.ds(base, count), k : k + 2 * LANES] = jnp.dot(
                normed, win_ref[:, inner + k : inner + k + 2 * LANES],
                preferred_element_type=jnp.float32,
            ).astype(jnp.bfloat16)

    for fetch in fetches:
        fetch.wait()
    spread_channels(rdecay, jnp.exp(-rrate_ref[...]), tiles)
    spread_channels(cdecay, jnp.exp(-crate_ref[...]), tiles)
    spread_channels(skip_tile, skip_ref[...], tiles)
    gate_part(tcol[c], c)

    zero = jnp.zeros((tiles, LANES), jnp.float32)
    lanes = 2 if share % 2 == 0 else 1

    def result_copy(q, k):
        g = (me + k) % group_n
        return pltpu.make_async_remote_copy(
            src_ref=rsend.at[q, pl.ds(g * piece_len, piece_len)],
            dst_ref=rrecv.at[q, pl.ds(me * piece_len, piece_len)],
            send_sem=rsend_sem.at[q, k], recv_sem=rrecv_sem.at[q],
            device_id=spot(g), device_id_type=MESH,
        )

    def row_chunk(q, _):
        pltpu.make_async_copy(tin.at[q], tin.at[q], tin_sem.at[q]).wait()
        normed = normalise(tin[q].astype(jnp.float32).reshape(chunk_len, width), gain_ref[...])
        mixers = transposed_dot(normed, wbc_ref[...])
        mixers = mixers.astype(jnp.bfloat16).astype(jnp.float32)
        spread_vectors(rb_ref, mixers, 0, states, 0)
        spread_vectors(rc_ref, mixers, states, states, 0)
        for k in range(0, tiles, 2):
            part = jnp.dot(normed, win_ref[:, k * LANES : (k + 2) * LANES],
                           preferred_element_type=jnp.float32)
            part = part.astype(jnp.bfloat16).astype(jnp.float32)
            for h in range(2):
                u_ref[pl.ds(k + h, chunk_len, stride=tiles), :] = part[:, h * LANES : (h + 1) * LANES]
        decay = [rdecay[n * tiles : (n + 1) * tiles, :] for n in range(states)]
        skip = skip_tile[...]

        def one_group(first, _):
            def one_step(j, carry):
                carry = list(carry)
                for w in range(columns):
                    for b in range(lanes):
                        row = first * lanes + b
                        patch = (j * share + row) * columns + w
                        owner = j * cols_n + w // per_core
                        value = u_ref[pl.ds(pl.multiple_of(patch * tiles, tiles), tiles), :]
                        carry[b], total = scan_step(carry[b], decay, value, rb_ref, rc_ref,
                                                    patch, skip * value, tiles)
                        rsend[q, (owner * share + row) * per_core + w % per_core] = total.astype(jnp.bfloat16)
                return tuple(carry)

            lax.fori_loop(0, rows_n, one_step, tuple((zero,) * states for _ in range(lanes)))
            return 0

        lax.fori_loop(0, share // lanes, one_group, 0)

        def send_result(k, _):
            result_copy(q, k).start()
            return 0

        pltpu.make_async_copy(
            rsend.at[q, pl.ds(me * piece_len, piece_len)],
            rrecv.at[q, pl.ds(me * piece_len, piece_len)], rrecv_sem.at[q],
        ).start()
        lax.fori_loop(1, group_n, send_result, 0)
        return 0

    lax.fori_loop(0, chunks, row_chunk, 0)

    for step in range(1, cols_n):
        column_copy(step).wait_recv()
        source = (c + cols_n - step) % cols_n
        gate_part(tcol[source], source)

    for g in range(per_core):
        for n in range(states):
            state_ref[g, n] = zero

    def out_copy(o):
        return pltpu.make_async_remote_copy(
            src_ref=stage.at[o], dst_ref=land.at[c, o % blocks_home],
            send_sem=osend_sem.at[o], recv_sem=orecv_sem.at[c, o % blocks_home],
            device_id={"cols": o // blocks_home}, device_id_type=MESH,
        )

    def col_chunk(q, _):
        pltpu.make_async_copy(rrecv.at[q], rrecv.at[q], rrecv_sem.at[q]).wait()
        decay = [cdecay[n * tiles : (n + 1) * tiles, :] for n in range(states)]
        base = q * chunk_len

        def one_step(s, carry):
            result = []
            for g in range(per_core):
                patch = s * per_core + g
                value = rrecv[q, patch].astype(jnp.float32)
                state, total = scan_step(carry[g], decay, value, cb_ref, cc_ref,
                                         base + patch, value, tiles)
                y_ref[pl.ds(pl.multiple_of(patch * tiles, tiles), tiles), :] = total
                result.append(state)
            return tuple(result)

        carry = tuple(tuple(state_ref[g, n] for n in range(states)) for g in range(per_core))
        carry = lax.fori_loop(0, chunk_len // per_core, one_step, carry)
        for g in range(per_core):
            for n in range(states):
                state_ref[g, n] = carry[g][n]
        start = pl.multiple_of(base, chunk_len)
        for t in range(tiles):
            gate = z_ref[pl.ds(start, chunk_len), t * LANES : (t + 1) * LANES].astype(jnp.float32)
            mixed = y_ref[pl.ds(t, chunk_len, stride=tiles), :]
            gated_ref[:, t * LANES : (t + 1) * LANES] = (
                mixed * (gate / (1.0 + jnp.exp(-gate)))
            ).astype(jnp.bfloat16)
        result = jnp.dot(gated_ref[...], wout_ref[...], preferred_element_type=jnp.float32)
        result = result.astype(jnp.bfloat16)
        for k in range(blocks // chunks):
            o = q * (blocks // chunks) + k
            block = result[k * block_len : (k + 1) * block_len]
            stage[o] = block

            @pl.when(o // blocks_home == c)
            def _():
                land[c, o % blocks_home] = block

            @pl.when(o // blocks_home != c)
            def _():
                out_copy(o).start()
        return 0

    lax.fori_loop(0, chunks, col_chunk, 0)

    def drain_tokens(k, _):
        g, copy = token_copy(k)

        @pl.when(g != me)
        def _():
            copy.wait_send()
        return 0

    lax.fori_loop(0, pieces, drain_tokens, 0)
    for step in range(1, cols_n):
        column_copy(step).wait_send()

    def drain_results(q, _):
        def one(k, _):
            result_copy(q, k).wait_send()
            return 0
        return lax.fori_loop(1, group_n, one, 0)

    lax.fori_loop(0, chunks, drain_results, 0)

    def drain_out(o, _):
        @pl.when(o // blocks_home != c)
        def _():
            out_copy(o).wait_send()
        return 0

    lax.fori_loop(0, blocks, drain_out, 0)
    for source in range(cols_n):
        @pl.when(source != c)
        def _():
            for i in range(blocks_home):
                pltpu.make_async_copy(
                    land.at[source, i], land.at[source, i], orecv_sem.at[source, i]
                ).wait()
    for i in range(blocks_home):
        parts = [
            land[s, i].astype(jnp.float32).reshape(block_len // per_core, per_core, -1)
            for s in range(cols_n)
        ]
        rows = block_len // per_core
        out_ref[i * rows : (i + 1) * rows] = jnp.concatenate(parts, axis=1).astype(jnp.bfloat16)


def per_device(tokens, norm_gain, w_in, w_bc, rate_row, rate_col, skip_gain, w_out):
    inner, width_out = w_out.shape
    states = rate_row.shape[0]
    height, columns, width = tokens.shape
    rows_n, cols_n = lax.axis_size("rows"), lax.axis_size("cols")
    group_n = rows_n * cols_n
    per_core = columns // cols_n
    total = height * cols_n
    share = min(4, total // group_n)
    chunks = total // (group_n * share)
    pieces = height // share
    piece_len = share * per_core
    chunk_len = group_n * piece_len
    tiles = inner // LANES
    blocks = max(chunks, cols_n)
    block_len = total * per_core // blocks
    patches = total * per_core
    f32, bf16 = jnp.float32, jnp.bfloat16
    dma = pltpu.SemaphoreType.DMA
    out = pl.pallas_call(
        functools.partial(layer_kernel, states, rows_n, cols_n, share, per_core),
        in_specs=[pl.BlockSpec(memory_space=pl.ANY)] * 8,
        out_specs=pl.BlockSpec(memory_space=pltpu.VMEM),
        out_shape=jax.ShapeDtypeStruct((height, columns, width_out), bf16),
        scratch_shapes=[
            pltpu.VMEM((1, width), f32),
            pltpu.VMEM(w_in.shape, bf16),
            pltpu.VMEM(w_bc.shape[::-1], bf16),
            pltpu.VMEM(rate_row.shape, f32),
            pltpu.VMEM(rate_col.shape, f32),
            pltpu.VMEM((1, inner), f32),
            pltpu.VMEM(w_out.shape, bf16),
            pltpu.VMEM((cols_n, height, columns, width), bf16),
            pltpu.VMEM((chunks, rows_n, share, columns, width), bf16),
            pltpu.VMEM((chunks, chunk_len, tiles, LANES), bf16),
            pltpu.VMEM((chunks, chunk_len, tiles, LANES), bf16),
            pltpu.VMEM((chunk_len * tiles, LANES), f32),
            pltpu.VMEM((states, chunk_len + 8, LANES), f32),
            pltpu.VMEM((states, chunk_len + 8, LANES), f32),
            pltpu.VMEM((states, patches + 8, LANES), f32),
            pltpu.VMEM((states, patches + 8, LANES), f32),
            pltpu.VMEM((patches, inner), bf16),
            pltpu.VMEM((chunk_len * tiles, LANES), f32),
            pltpu.VMEM((chunk_len, inner), bf16),
            pltpu.VMEM((states * tiles, LANES), f32),
            pltpu.VMEM((states * tiles, LANES), f32),
            pltpu.VMEM((tiles, LANES), f32),
            pltpu.VMEM((blocks, block_len, width_out), bf16),
            pltpu.VMEM((cols_n, blocks // cols_n, block_len, width_out), bf16),
            pltpu.VMEM((per_core, states, tiles, LANES), f32),
            dma((pieces,)), dma((chunks,)), dma((cols_n,)), dma((cols_n,)),
            dma((chunks, group_n)), dma((chunks,)), dma((blocks,)),
            dma((cols_n, blocks // cols_n)), dma((8,)),
        ],
        compiler_params=pltpu.CompilerParams(
            vmem_limit_bytes=VMEM_LIMIT, collective_id=0, has_side_effects=True
        ),
        name="layer",
    )(tokens, norm_gain[None], w_in, w_bc.T, rate_row, rate_col, skip_gain[None], w_out)
    return out


def solution(mesh):
    placed = (P(("slides", "cols"), "rows", None), P(), P(), P(), P(), P(), P(), P())
    return jax.shard_map(
        per_device,
        mesh=mesh,
        in_specs=placed,
        out_specs=P(("slides", "cols"), "rows", None),
        check_vma=False,
    )
```
